32 devices in a mesh: dp: 8 (over z, core), tensor: 4 (over y, x).
Axes of the slice: x: 2, y: 2, z: 4, core: 2. Of those that a mesh axis runs over, the one named last changes fastest.
Arguments:
- block_input: bfloat16 [8192, 2048], P(('dp', 'tensor')), may hold values from -6 to 6
- cotangent: bfloat16 [8192, 2048], P(('dp', 'tensor')), may hold values from -6 to 6
- sequence_lengths: int32 [32], replicated, may hold values from 1 to 512, as said below
- sequence_owner: int32 [32], replicated, may hold values from 0 to 7, as said below
- sequence_offset: int32 [32], replicated, may hold values from 0 to 1023, as said below
- query_key: float32 [2, 2048, 2048], P(None, 'dp', 'tensor'), may hold values from -1 to 1
- value_gate: float32 [2, 2048, 4096], P(None, 'dp', 'tensor'), may hold values from -0.125 to 0.125
- output_weight: float32 [4096, 2048], P('tensor', 'dp'), may hold values from -0.1875 to 0.1875
- feed_in: float32 [2, 2048, 4096], P(None, 'dp', 'tensor'), may hold values from -0.125 to 0.125
- feed_out: float32 [4096, 2048], P('tensor', 'dp'), may hold values from -0.1875 to 0.1875
- mean_query_key: float32 [2, 2048, 2048], P(None, 'dp', 'tensor'), may hold values from -6 to 6
- mean_value_gate: float32 [2, 2048, 4096], P(None, 'dp', 'tensor'), may hold values from -6 to 6
- mean_output_weight: float32 [4096, 2048], P('tensor', 'dp'), may hold values from -6 to 6
- mean_feed_in: float32 [2, 2048, 4096], P(None, 'dp', 'tensor'), may hold values from -6 to 6
- mean_feed_out: float32 [4096, 2048], P('tensor', 'dp'), may hold values from -6 to 6
- square_query_key: float32 [2, 2048, 2048], P(None, 'dp', 'tensor'), may hold values from 0.01 to 10
- square_value_gate: float32 [2, 2048, 4096], P(None, 'dp', 'tensor'), may hold values from 0.01 to 10
- square_output_weight: float32 [4096, 2048], P('tensor', 'dp'), may hold values from 0.01 to 10
- square_feed_in: float32 [2, 2048, 4096], P(None, 'dp', 'tensor'), may hold values from 0.01 to 10
- square_feed_out: float32 [4096, 2048], P('tensor', 'dp'), may hold values from 0.01 to 10
Outputs:
- block_output: bfloat16 [8192, 2048], P(('dp', 'tensor'))
- input_gradient: float32 [8192, 2048], P(('dp', 'tensor'))
- gradient_query_key: float32 [2, 2048, 2048], P(None, 'dp', 'tensor')
- gradient_value_gate: float32 [2, 2048, 4096], P(None, 'dp', 'tensor')
- gradient_output_weight: float32 [4096, 2048], P('tensor', 'dp')
- gradient_feed_in: float32 [2, 2048, 4096], P(None, 'dp', 'tensor')
- gradient_feed_out: float32 [4096, 2048], P('tensor', 'dp')
- updated_query_key: float32 [2, 2048, 2048], P(None, 'dp', 'tensor')
- updated_value_gate: float32 [2, 2048, 4096], P(None, 'dp', 'tensor')
- updated_output_weight: float32 [4096, 2048], P('tensor', 'dp')
- updated_feed_in: float32 [2, 2048, 4096], P(None, 'dp', 'tensor')
- updated_feed_out: float32 [4096, 2048], P('tensor', 'dp')
- updated_mean_query_key: float32 [2, 2048, 2048], P(None, 'dp', 'tensor')
- updated_mean_value_gate: float32 [2, 2048, 4096], P(None, 'dp', 'tensor')
- updated_mean_output_weight: float32 [4096, 2048], P('tensor', 'dp')
- updated_mean_feed_in: float32 [2, 2048, 4096], P(None, 'dp', 'tensor')
- updated_mean_feed_out: float32 [4096, 2048], P('tensor', 'dp')
- updated_square_query_key: float32 [2, 2048, 2048], P(None, 'dp', 'tensor')
- updated_square_value_gate: float32 [2, 2048, 4096], P(None, 'dp', 'tensor')
- updated_square_output_weight: float32 [4096, 2048], P('tensor', 'dp')
- updated_square_feed_in: float32 [2, 2048, 4096], P(None, 'dp', 'tensor')
- updated_square_feed_out: float32 [4096, 2048], P('tensor', 'dp')
The draws below stay inside these ranges and needn't reach their ends.
Inputs may be any that keep to these rules, and one draw needn't show every extreme that they name: `sequence_lengths`: every buffer holds 4 sequences whose lengths add up to at most 1024; in one buffer they add up to exactly 1024. `sequence_owner`: every index of dp owns exactly 4 sequences. `sequence_offset`: A sequence's offset is the sum of the lengths of the lower-numbered sequences in the same buffer, so a buffer's sequences lie packed from its first row in order of their number.
All inputs are finite; a program needn't handle non-finite values.
Results may differ from the reference program's by a relative error of at most 0.028.
Values may be sent and summed in bfloat16 or wider, within the bound.
No kernel may reach another device: no remote copies, remote signals or barrier semaphores. Data moves between devices by JAX's collectives and lax.ppermute only.
A program may use at most 320 MiB of HBM per device.

```python
import math
import jax
import jax.numpy as jnp
from jax import lax

D = 2048
HEADS = 8
DK = 256
DV = 512
FF = 4096
ROWS = 1024
SPD = 4
TOKENS = 8192
SEQS = 32
N_DP = 8
N_TENSOR = 4


def sequence_tables(key):
    owners_count = SEQS // SPD
    base = jax.random.fold_in(key, 4242)
    slot_key, short_key, middle_key, full_key = jax.random.split(base, 4)
    slots = jax.random.permutation(slot_key, SEQS).astype(jnp.int32)
    owner = (slots // SPD).astype(jnp.int32)
    numbers = jnp.arange(SEQS, dtype=jnp.int32)
    same = owner[:, None] == owner[None, :]
    before = numbers[None, :] < numbers[:, None]
    local = jnp.sum((same & before).astype(jnp.int32), axis=1).astype(jnp.int32)
    short = jax.random.randint(short_key, (owners_count, SPD), 1, ROWS // 5 + 1, dtype=jnp.int32)
    middle = jax.random.randint(middle_key, (), 1, ROWS // 6 + 1, dtype=jnp.int32)
    fullest = jax.random.randint(full_key, (), 0, owners_count, dtype=jnp.int32)
    longest = jnp.full((), ROWS // 2, jnp.int32)
    single_row = jnp.ones((), jnp.int32)
    full_row = jnp.stack([longest, middle, longest - single_row - middle, single_row]).astype(jnp.int32)
    table = jnp.where(jnp.arange(owners_count, dtype=jnp.int32)[:, None] == fullest, full_row[None, :], short)
    lengths = table[owner, local].astype(jnp.int32)
    offsets = jnp.sum(jnp.where(same & before, lengths[None, :], 0), axis=1).astype(jnp.int32)
    return (lengths, owner, offsets)


def draw_sequence_lengths(key, part):
    return sequence_tables(key)[0]


def draw_sequence_owner(key, part):
    return sequence_tables(key)[1]


def draw_sequence_offset(key, part):
    return sequence_tables(key)[2]


def draw_query_key(key, part):
    shared_key, extra_key = jax.random.split(jax.random.fold_in(key, 777), 2)
    shape = (D, HEADS * DK)
    shared = jnp.clip(jax.random.normal(shared_key, shape, jnp.float32), -4.0, 4.0)
    extra = jnp.clip(jax.random.normal(extra_key, shape, jnp.float32), -4.0, 4.0)
    scale = D ** (-0.5)
    query_part = shared * scale
    key_part = (shared + 0.5 * extra) * scale
    return jnp.stack([query_part, key_part]).astype(jnp.float32)


def block_levels(rng, extent, shards, smallest, high):
    loudness = 1.0
    for dim, shards_of in shards:
        steps = jax.random.uniform(jax.random.fold_in(jax.random.fold_in(rng, 6), dim), (shards_of,), jnp.float32, smallest / len(shards), high / len(shards))
        loudness = loudness * jnp.repeat(jnp.exp(steps), extent[dim] // shards_of).reshape((-1,) + (1,) * (len(extent) - 1 - dim))
    return loudness


def noise(stream_key, extent, scale, most, shards=(), kind=jnp.bfloat16):
    result = jax.random.normal(stream_key, extent, jnp.float32) * scale
    if len(shards) > 0:
        result = block_levels(stream_key, extent, shards, -0.22, 0.18) * result
    return jnp.clip(result, min=-most, max=most).astype(kind)


def setup_inputs(seed: int = 0) -> dict:
    arg_keys = jax.random.split(jax.random.key(seed), 21)
    block_input = noise(arg_keys[0], (TOKENS, D), 1.0, 6.0, ((0, 32),))
    cotangent = noise(arg_keys[1], (TOKENS, D), 1.0, 6.0, ((0, 32),))
    sequence_lengths = draw_sequence_lengths(jax.random.fold_in(arg_keys[20], 71), 0)
    sequence_owner = draw_sequence_owner(jax.random.fold_in(arg_keys[20], 71), 0)
    sequence_offset = draw_sequence_offset(jax.random.fold_in(arg_keys[20], 71), 0)
    query_key = draw_query_key(jax.random.fold_in(arg_keys[20], 71), 0)
    value_gate = noise(arg_keys[6], (2, D, HEADS * DV), D ** -0.5, 0.125, ((1, 8), (2, 4)), jnp.float32)
    output_weight = noise(arg_keys[7], (HEADS * DV, D), (HEADS * DV // 4) ** -0.5, 0.1875, ((0, 4), (1, 8)), jnp.float32)
    feed_in = noise(arg_keys[8], (2, D, FF), D ** -0.5, 0.125, ((1, 8), (2, 4)), jnp.float32)
    feed_out = noise(arg_keys[9], (FF, D), (FF // 4) ** -0.5, 0.1875, ((0, 4), (1, 8)), jnp.float32)
    mean_query_key = noise(arg_keys[10], (2, D, HEADS * DK), 1.0, 6.0, ((1, 8), (2, 4)), jnp.float32)
    mean_value_gate = noise(arg_keys[11], (2, D, HEADS * DV), 1.0, 6.0, ((1, 8), (2, 4)), jnp.float32)
    mean_output_weight = noise(arg_keys[12], (HEADS * DV, D), 1.0, 6.0, ((0, 4), (1, 8)), jnp.float32)
    mean_feed_in = noise(arg_keys[13], (2, D, FF), 1.0, 6.0, ((1, 8), (2, 4)), jnp.float32)
    mean_feed_out = noise(arg_keys[14], (FF, D), 1.0, 6.0, ((0, 4), (1, 8)), jnp.float32)
    square_query_key = jnp.clip(jnp.exp(math.log(10.0) - 6.9077553 * jax.random.uniform(arg_keys[15], (2, D, HEADS * DK), jnp.float32) ** block_levels(arg_keys[15], (2, D, HEADS * DK), ((1, 8), (2, 4)), -0.2, 0.2)), 0.01, 10.0)
    square_value_gate = jnp.clip(jnp.exp(math.log(10.0) - 6.9077553 * jax.random.uniform(arg_keys[16], (2, D, HEADS * DV), jnp.float32) ** block_levels(arg_keys[16], (2, D, HEADS * DV), ((1, 8), (2, 4)), -0.2, 0.2)), 0.01, 10.0)
    square_output_weight = jnp.clip(jnp.exp(math.log(10.0) - 6.9077553 * jax.random.uniform(arg_keys[17], (HEADS * DV, D), jnp.float32) ** block_levels(arg_keys[17], (HEADS * DV, D), ((0, 4), (1, 8)), -0.2, 0.2)), 0.01, 10.0)
    square_feed_in = jnp.clip(jnp.exp(math.log(10.0) - 6.9077553 * jax.random.uniform(arg_keys[18], (2, D, FF), jnp.float32) ** block_levels(arg_keys[18], (2, D, FF), ((1, 8), (2, 4)), -0.2, 0.2)), 0.01, 10.0)
    square_feed_out = jnp.clip(jnp.exp(math.log(10.0) - 6.9077553 * jax.random.uniform(arg_keys[19], (FF, D), jnp.float32) ** block_levels(arg_keys[19], (FF, D), ((0, 4), (1, 8)), -0.2, 0.2)), 0.01, 10.0)
    return dict(block_input=block_input, cotangent=cotangent, sequence_lengths=sequence_lengths, sequence_owner=sequence_owner, sequence_offset=sequence_offset, query_key=query_key, value_gate=value_gate, output_weight=output_weight, feed_in=feed_in, feed_out=feed_out, mean_query_key=mean_query_key, mean_value_gate=mean_value_gate, mean_output_weight=mean_output_weight, mean_feed_in=mean_feed_in, mean_feed_out=mean_feed_out, square_query_key=square_query_key, square_value_gate=square_value_gate, square_output_weight=square_output_weight, square_feed_in=square_feed_in, square_feed_out=square_feed_out)


EPS_NORM = 1e-06
EPS_GROUP = 1e-05
LEARN_RATE = 0.01
BETA_FIRST = 0.9
BETA_SECOND = 0.999
ADAM_EPS = 1e-08
WEIGHT_DECAY = 0.1
step_count = 3

def row_tables(lengths, owners, offsets, buffer, rows):
    numbers = jnp.arange(lengths.shape[0], dtype=jnp.int32)
    inside = (owners[None, :] == buffer) & (rows[:, None] >= offsets[None, :]) & (rows[:, None] < offsets[None, :] + lengths[None, :])
    inside = inside.astype(jnp.int32)
    segment = (lax.optimization_barrier(jnp.sum(inside * (numbers[None, :] + 1), axis=1)) - 1).astype(jnp.int32)
    position = lax.optimization_barrier(jnp.sum(inside * (rows[:, None] - offsets[None, :]), axis=1)).astype(jnp.int32)
    valid = lax.optimization_barrier(jnp.sum(inside, axis=1)).astype(jnp.int32)
    return (segment, position, valid)

def rotary_tables(position, half):
    ladder = jnp.exp(-math.log(10000.0) * jnp.arange(half, dtype=jnp.float32) / half)
    angle = position.astype(jnp.float32)[:, None] * ladder[None, :]
    return (jnp.cos(angle), jnp.sin(angle))

def rotate(value, cosine, sine):
    half = value.shape[-1] // 2
    first = value[..., :half]
    second = value[..., half:]
    cosines = cosine[:, None, :]
    sines = sine[:, None, :]
    return jnp.concatenate([first * cosines - second * sines, second * cosines + first * sines], axis=-1)

def rotate_back(value, cosine, sine):
    half = value.shape[-1] // 2
    first = value[..., :half]
    second = value[..., half:]
    cosines = cosine[:, None, :]
    sines = sine[:, None, :]
    return jnp.concatenate([first * cosines + second * sines, second * cosines - first * sines], axis=-1)

def decay_tile(segment_rows, place_rows, segment_cols, place_cols, log_gamma):
    linked = (segment_rows[:, None] == segment_cols[None, :]) & (segment_rows[:, None] >= 0) & (place_cols[None, :] <= place_rows[:, None])
    spacing = jnp.maximum(place_rows[:, None] - place_cols[None, :], 0).astype(jnp.float32)
    return jnp.where(linked[None], jnp.exp(spacing[None] * log_gamma[:, None, None]), 0.0)

def group_terms(left, right):
    width = left.shape[1] // N_TENSOR
    left_groups = left.astype(jnp.float32).reshape(left.shape[0], N_TENSOR, width)
    right_groups = right.astype(jnp.float32).reshape(N_TENSOR, width, right.shape[1])
    return jnp.einsum('rgc,gcd->grd', left_groups, right_groups)

def rounded_total(terms):
    rounded = lax.optimization_barrier(terms.astype(jnp.bfloat16))
    return lax.optimization_barrier(jnp.sum(rounded.astype(jnp.float32), axis=0))

def contract_rows(left, right):
    return lax.dot_general(left, right, (((0,), (0,)), ((), ())), preferred_element_type=jnp.float32)

def adam_update(weight, first, second, slope):
    first_new = BETA_FIRST * first + (1.0 - BETA_FIRST) * slope
    second_new = BETA_SECOND * second + (1.0 - BETA_SECOND) * slope * slope
    first_hat = first_new / (1.0 - BETA_FIRST ** step_count)
    second_hat = second_new / (1.0 - BETA_SECOND ** step_count)
    weight_new = weight - LEARN_RATE * (first_hat / (jnp.sqrt(second_hat) + ADAM_EPS) + WEIGHT_DECAY * weight)
    return (weight_new, first_new, second_new)

def reference(block_input, cotangent, sequence_lengths, sequence_owner, sequence_offset, query_key, value_gate, output_weight, feed_in, feed_out, mean_query_key, mean_value_gate, mean_output_weight, mean_feed_in, mean_feed_out, square_query_key, square_value_gate, square_output_weight, square_feed_in, square_feed_out):
    half_bits = jnp.bfloat16
    single = jnp.float32
    weight_query = query_key[0].astype(half_bits)
    weight_key = query_key[1].astype(half_bits)
    weight_value = value_gate[0].astype(half_bits)
    weight_gate = value_gate[1].astype(half_bits)
    weight_out = output_weight.astype(half_bits)
    weight_up_gate = feed_in[0].astype(half_bits)
    weight_up_line = feed_in[1].astype(half_bits)
    weight_down = feed_out.astype(half_bits)
    log_gamma = jnp.log(1.0 - jnp.exp2(-5.0 - jnp.arange(HEADS, dtype=single)))
    rows = jnp.arange(ROWS, dtype=jnp.int32)
    sqrt_two = math.sqrt(2.0)
    density = 1.0 / math.sqrt(2.0 * math.pi)

    def one_buffer(carry, inputs):
        input_rows, grad_out_rows, buffer = inputs
        segment, position, valid = row_tables(sequence_lengths, sequence_owner, sequence_offset, buffer, rows)
        valid_rows = valid.astype(single)[:, None]
        cosine, sine = rotary_tables(position, DK // 2)
        inputs_f = input_rows.astype(single)
        in_scale = lax.rsqrt(lax.optimization_barrier(jnp.mean(inputs_f * inputs_f, axis=1, keepdims=True)) + EPS_NORM)
        normed_in = (inputs_f * in_scale).astype(half_bits)
        query_raw = jnp.dot(normed_in, weight_query, preferred_element_type=single).reshape(ROWS, HEADS, DK)
        key_raw = jnp.dot(normed_in, weight_key, preferred_element_type=single).reshape(ROWS, HEADS, DK)
        values = jnp.dot(normed_in, weight_value, preferred_element_type=single).astype(half_bits).reshape(ROWS, HEADS, DV)
        gate = jnp.dot(normed_in, weight_gate, preferred_element_type=single)
        query_rot = rotate(query_raw, cosine, sine).astype(half_bits)
        key_rot = (rotate(key_raw, cosine, sine) * DK ** (-0.5)).astype(half_bits)
        decay = decay_tile(segment, position, segment, position, log_gamma)
        scores = (jnp.einsum('ihd,jhd->hij', query_rot.astype(single), key_rot.astype(single)) * decay).astype(half_bits)
        mixed = jnp.einsum('hij,jhc->ihc', scores.astype(single), values.astype(single))
        group_scale = lax.rsqrt(lax.optimization_barrier(jnp.mean(mixed * mixed, axis=2, keepdims=True)) + EPS_GROUP)
        normed_mix = (mixed * group_scale).reshape(ROWS, HEADS * DV)
        swish = jax.nn.silu(gate)
        gated = (swish * normed_mix).astype(half_bits)
        hidden_state = inputs_f + rounded_total(group_terms(gated, weight_out))
        mid_scale = lax.rsqrt(lax.optimization_barrier(jnp.mean(hidden_state * hidden_state, axis=1, keepdims=True)) + EPS_NORM)
        normed_mid = (hidden_state * mid_scale).astype(half_bits)
        up_gate = jnp.dot(normed_mid, weight_up_gate, preferred_element_type=single)
        up_line = jnp.dot(normed_mid, weight_up_line, preferred_element_type=single)
        normal_cdf = 0.5 * (1.0 + lax.erf(up_gate / sqrt_two))
        activated = up_gate * normal_cdf
        expanded = (activated * up_line).astype(half_bits)
        block_rows = hidden_state + valid_rows * rounded_total(group_terms(expanded, weight_down))
        grad_out_f = grad_out_rows.astype(single)
        grad_branch = (valid_rows * grad_out_f).astype(half_bits)
        grad_expanded = jnp.dot(grad_branch, weight_down.T, preferred_element_type=single)
        slope_down = contract_rows(expanded, grad_branch)
        normal_pdf = density * jnp.exp(-0.5 * up_gate * up_gate)
        grad_up_gate = (grad_expanded * up_line * (normal_cdf + up_gate * normal_pdf)).astype(half_bits)
        grad_up_line = (grad_expanded * activated).astype(half_bits)
        slope_feed_in = jnp.stack([contract_rows(normed_mid, grad_up_gate), contract_rows(normed_mid, grad_up_line)])
        grad_mid = rounded_total(group_terms(grad_up_gate, weight_up_gate.T) + group_terms(grad_up_line, weight_up_line.T))
        grad_hidden = grad_out_f + mid_scale * grad_mid - hidden_state * mid_scale ** 3 * lax.optimization_barrier(jnp.mean(grad_mid * hidden_state, axis=1, keepdims=True))
        grad_rows = grad_hidden.astype(half_bits)
        grad_gated = jnp.dot(grad_rows, weight_out.T, preferred_element_type=single)
        slope_out = contract_rows(gated, grad_rows)
        sigma = jax.nn.sigmoid(gate)
        grad_gate = (grad_gated * normed_mix * sigma * (1.0 + gate * (1.0 - sigma))).astype(half_bits)
        grad_normed = (grad_gated * swish).reshape(ROWS, HEADS, DV)
        grad_mixed = (group_scale * grad_normed - mixed * group_scale ** 3 * lax.optimization_barrier(jnp.mean(grad_normed * mixed, axis=2, keepdims=True))).astype(half_bits)
        grad_scores = (jnp.einsum('ihc,jhc->hij', grad_mixed.astype(single), values.astype(single)) * decay).astype(half_bits)
        grad_query_rot = jnp.einsum('hij,jhd->ihd', grad_scores.astype(single), key_rot.astype(single))
        grad_key_rot = jnp.einsum('hij,ihd->jhd', grad_scores.astype(single), query_rot.astype(single))
        grad_values = jnp.einsum('hij,ihc->jhc', scores.astype(single), grad_mixed.astype(single))
        grad_query = rotate_back(grad_query_rot, cosine, sine).astype(half_bits).reshape(ROWS, HEADS * DK)
        grad_key = (rotate_back(grad_key_rot, cosine, sine) * DK ** (-0.5)).astype(half_bits).reshape(ROWS, HEADS * DK)
        grad_value = grad_values.astype(half_bits).reshape(ROWS, HEADS * DV)
        slope_query_key = jnp.stack([contract_rows(normed_in, grad_query), contract_rows(normed_in, grad_key)])
        slope_value_gate = jnp.stack([contract_rows(normed_in, grad_value), contract_rows(normed_in, grad_gate)])
        grad_in = rounded_total(group_terms(grad_query, weight_query.T) + group_terms(grad_key, weight_key.T) + group_terms(grad_value, weight_value.T) + group_terms(grad_gate, weight_gate.T))
        input_rows_grad = grad_hidden + in_scale * grad_in - inputs_f * in_scale ** 3 * lax.optimization_barrier(jnp.mean(grad_in * inputs_f, axis=1, keepdims=True))
        slopes = (slope_query_key, slope_value_gate, slope_out, slope_feed_in, slope_down)
        carry = jax.tree.map(lambda total, part: total + part, carry, slopes)
        return (carry, (block_rows.astype(half_bits), input_rows_grad))
    start = (jnp.zeros(query_key.shape, single), jnp.zeros(value_gate.shape, single), jnp.zeros(output_weight.shape, single), jnp.zeros(feed_in.shape, single), jnp.zeros(feed_out.shape, single))
    stacked = (block_input.reshape(N_DP, ROWS, D), cotangent.reshape(N_DP, ROWS, D), jnp.arange(N_DP, dtype=jnp.int32))
    slopes, outputs = lax.scan(one_buffer, start, stacked)
    block_output = outputs[0].reshape(N_DP * ROWS, D)
    input_gradient = outputs[1].reshape(N_DP * ROWS, D)
    new_qk = adam_update(query_key, mean_query_key, square_query_key, slopes[0])
    new_vg = adam_update(value_gate, mean_value_gate, square_value_gate, slopes[1])
    new_out = adam_update(output_weight, mean_output_weight, square_output_weight, slopes[2])
    new_in = adam_update(feed_in, mean_feed_in, square_feed_in, slopes[3])
    new_down = adam_update(feed_out, mean_feed_out, square_feed_out, slopes[4])
    return (block_output, input_gradient, slopes[0], slopes[1], slopes[2], slopes[3], slopes[4], new_qk[0], new_vg[0], new_out[0], new_in[0], new_down[0], new_qk[1], new_vg[1], new_out[1], new_in[1], new_down[1], new_qk[2], new_vg[2], new_out[2], new_in[2], new_down[2])
```

```python
import functools
import math

import jax
import jax.numpy as jnp
from jax import lax
from jax.experimental import pallas as pl
from jax.experimental.pallas import tpu as pltpu
from jax.sharding import PartitionSpec as P

DK = 256
DV = 512
HEAD = 2 * DK + 2 * DV

EPS_NORM = 1e-06
EPS_GROUP = 1e-05
LEARN_RATE = 0.01
BETA_FIRST = 0.9
BETA_SECOND = 0.999
ADAM_EPS = 1e-08
WEIGHT_DECAY = 0.1
step_count = 3


BF = jnp.bfloat16
F32 = jnp.float32


def row_tables(lengths, owners, offsets, buffer, rows):
    numbers = jnp.arange(lengths.shape[0], dtype=jnp.int32)
    inside = (
        (owners[None, :] == buffer)
        & (rows[:, None] >= offsets[None, :])
        & (rows[:, None] < offsets[None, :] + lengths[None, :])
    )
    inside = inside.astype(jnp.int32)
    segment = jnp.sum(inside * (numbers[None, :] + 1), axis=1) - 1
    position = jnp.sum(inside * (rows[:, None] - offsets[None, :]), axis=1)
    valid = jnp.sum(inside, axis=1)
    return (segment, position, valid)


def rotary_tables(position, half):
    ladder = jnp.exp(-math.log(10000.0) * jnp.arange(half, dtype=F32) / half)
    angle = position.astype(F32)[:, None] * ladder[None, :]
    return (jnp.cos(angle), jnp.sin(angle))


def contract_rows(left, right, kind=BF):
    return lax.dot_general(
        left, right, (((0,), (0,)), ((), ())), preferred_element_type=F32
    ).astype(kind)


def times(left, right):
    return lax.dot_general(left, right, (((1,), (0,)), ((), ())), preferred_element_type=F32)


def times_t(left, right):
    return lax.dot_general(left, right, (((1,), (1,)), ((), ())), preferred_element_type=F32)


def adam_update(weight, first, second, slope):
    first_new = BETA_FIRST * first + (1.0 - BETA_FIRST) * slope
    second_new = BETA_SECOND * second + (1.0 - BETA_SECOND) * slope * slope
    first_hat = first_new / (1.0 - BETA_FIRST**step_count)
    second_hat = second_new / (1.0 - BETA_SECOND**step_count)
    weight_new = weight - LEARN_RATE * (
        first_hat / (jnp.sqrt(second_hat) + ADAM_EPS) + WEIGHT_DECAY * weight
    )
    return (weight_new, first_new, second_new)


def swap(block, k, tensors):
    return lax.ppermute(block, "tensor", [(i, i ^ k) for i in range(tensors)])


def gather_blocks(block, tensors):
    order = list(range(tensors - 1, 0, -1))
    got = {0: block}
    for k in order:
        got[k] = swap(block, k, tensors)
    return jnp.concatenate([got[k] for k in range(tensors)], axis=0)


def scatter_blocks(make, tensors):
    total = None
    got = []
    for k in range(tensors - 1, 0, -1):
        got.append(swap(make(k).astype(BF), k, tensors))
    total = make(0).astype(BF).astype(F32)
    for part in got:
        total = total + part.astype(F32)
    return total


def decay_of(seg_rows, pos_rows, seg_cols, pos_cols, log_gamma):
    linked = (seg_rows == seg_cols) & (seg_rows >= 0) & (pos_cols <= pos_rows)
    spacing = jnp.maximum(pos_rows - pos_cols, 0).astype(F32)
    return jnp.where(linked, jnp.exp(spacing * log_gamma), 0.0)


def forward_kernel(blocks, active, gammas, proj, cos, sin, segc, posc, segr, posr,
                   query, key, value, mixed, gated):
    size = proj.shape[0] // blocks
    half = DK // 2
    log_gamma = gammas[pl.program_id(0)]

    def spin(index, carry):
        rows = pl.ds(pl.multiple_of(index * size, size), size)
        c = cos[rows, :]
        s = sin[rows, :]
        a = proj[rows, 0:half]
        b = proj[rows, half:DK]
        query[rows, 0:half] = (a * c - b * s).astype(BF)
        query[rows, half:DK] = (b * c + a * s).astype(BF)
        a = proj[rows, DK : DK + half]
        b = proj[rows, DK + half : 2 * DK]
        key[rows, 0:half] = ((a * c - b * s) * DK ** (-0.5)).astype(BF)
        key[rows, half:DK] = ((b * c + a * s) * DK ** (-0.5)).astype(BF)
        value[rows, :] = proj[rows, 2 * DK : 2 * DK + DV].astype(BF)
        mixed[rows, :] = jnp.zeros((size, DV), F32)
        return carry

    lax.fori_loop(0, blocks, spin, 0)

    def query_block(qi, carry):
        rows = pl.ds(pl.multiple_of(qi * size, size), size)
        for ki in range(blocks):
            cols = slice(ki * size, (ki + 1) * size)

            @pl.when(active[qi * blocks + ki] != 0)
            def _():
                decay = decay_of(
                    segc[rows, :], posc[rows, :], segr[:, cols], posr[:, cols], log_gamma
                )
                scores = (times_t(query[rows, :], key[cols, :]) * decay).astype(BF)
                mixed[rows, :] += times(scores, value[cols, :])

        total = mixed[rows, :]
        scale = lax.rsqrt(jnp.mean(total * total, axis=1, keepdims=True) + EPS_GROUP)
        gate = proj[rows, 2 * DK + DV : HEAD]
        gated[rows, :] = (gate * jax.nn.sigmoid(gate) * (total * scale)).astype(BF)
        return carry

    lax.fori_loop(0, blocks, query_block, 0)


def backward_kernel(blocks, active, gammas, query, key, value, mixed, gate_ref, grad_gated,
                    cos, sin, segc, posc, segr, posr, out, grad_mixed, grad_q, grad_k, grad_v):
    size = query.shape[0] // blocks
    half = DK // 2
    log_gamma = gammas[pl.program_id(0)]

    def prepare(index, carry):
        rows = pl.ds(pl.multiple_of(index * size, size), size)
        total = mixed[rows, :]
        gate = gate_ref[rows, :]
        slope = grad_gated[rows, :]
        scale = lax.rsqrt(jnp.mean(total * total, axis=1, keepdims=True) + EPS_GROUP)
        sigma = jax.nn.sigmoid(gate)
        out[rows, 2 * DK + DV : HEAD] = (
            slope * (total * scale) * sigma * (1.0 + gate * (1.0 - sigma))
        ).astype(BF)
        normed = slope * (gate * sigma)
        grad_mixed[rows, :] = (
            scale * normed
            - total * (scale * scale * scale) * jnp.mean(normed * total, axis=1, keepdims=True)
        ).astype(BF)
        grad_q[rows, :] = jnp.zeros((size, DK), F32)
        grad_k[rows, :] = jnp.zeros((size, DK), F32)
        grad_v[rows, :] = jnp.zeros((size, DV), F32)
        return carry

    lax.fori_loop(0, blocks, prepare, 0)

    def query_block(qi, carry):
        rows = pl.ds(pl.multiple_of(qi * size, size), size)
        for ki in range(blocks):
            cols = slice(ki * size, (ki + 1) * size)

            @pl.when(active[qi * blocks + ki] != 0)
            def _():
                decay = decay_of(
                    segc[rows, :], posc[rows, :], segr[:, cols], posr[:, cols], log_gamma
                )
                q = query[rows, :]
                k = key[cols, :]
                slope = grad_mixed[rows, :]
                scores = (times_t(q, k) * decay).astype(BF)
                grad_scores = (times_t(slope, value[cols, :]) * decay).astype(BF)
                grad_q[rows, :] += times(grad_scores, k)
                grad_k[cols, :] += contract_rows(grad_scores, q, F32)
                grad_v[cols, :] += contract_rows(scores, slope, F32)

        return carry

    lax.fori_loop(0, blocks, query_block, 0)

    def finish(index, carry):
        rows = pl.ds(pl.multiple_of(index * size, size), size)
        c = cos[rows, :]
        s = sin[rows, :]
        a = grad_q[rows, 0:half]
        b = grad_q[rows, half:DK]
        out[rows, 0:half] = (a * c + b * s).astype(BF)
        out[rows, half:DK] = (b * c - a * s).astype(BF)
        a = grad_k[rows, 0:half]
        b = grad_k[rows, half:DK]
        out[rows, DK : DK + half] = ((a * c + b * s) * DK ** (-0.5)).astype(BF)
        out[rows, DK + half : 2 * DK] = ((b * c - a * s) * DK ** (-0.5)).astype(BF)
        out[rows, 2 * DK : 2 * DK + DV] = grad_v[rows, :].astype(BF)
        return carry

    lax.fori_loop(0, blocks, finish, 0)


def whole_block(shape):
    return pl.BlockSpec(shape, lambda h, *_: (0, 0))


def head_block(rows, width, scale=1, shift=0):
    return pl.BlockSpec((rows, width), lambda h, *_: (0, h * scale + shift))


def table_specs(rows):
    return [
        whole_block((rows, DK // 2)),
        whole_block((rows, DK // 2)),
        whole_block((rows, 1)),
        whole_block((rows, 1)),
        whole_block((1, rows)),
        whole_block((1, rows)),
    ]


def retention_forward(proj, tables, active, gammas, blocks):
    rows, width = proj.shape
    heads = width // HEAD
    pairs = rows * rows // 2 * heads
    return pl.pallas_call(
        functools.partial(forward_kernel, blocks),
        out_shape=(
            jax.ShapeDtypeStruct((rows, heads * DK), BF),
            jax.ShapeDtypeStruct((rows, heads * DK), BF),
            jax.ShapeDtypeStruct((rows, heads * DV), BF),
            jax.ShapeDtypeStruct((rows, heads * DV), F32),
            jax.ShapeDtypeStruct((rows, heads * DV), BF),
        ),
        grid_spec=pltpu.PrefetchScalarGridSpec(
            num_scalar_prefetch=2,
            grid=(heads,),
            in_specs=[head_block(rows, HEAD)] + table_specs(rows),
            out_specs=(
                head_block(rows, DK),
                head_block(rows, DK),
                head_block(rows, DV),
                head_block(rows, DV),
                head_block(rows, DV),
            ),
        ),
        compiler_params=pltpu.CompilerParams(vmem_limit_bytes=56 << 20),
        cost_estimate=pl.CostEstimate(
            flops=pairs * (DK + DV) * 2,
            transcendentals=pairs,
            bytes_accessed=rows * heads * (HEAD * 4 + DK * 4 + DV * 8),
        ),
        name="retention_forward",
    )(active, gammas, proj, *tables)


def retention_backward(query, key, value, mixed, proj, grad_gated, tables, active, gammas, blocks):
    rows = query.shape[0]
    heads = query.shape[1] // DK
    pairs = rows * rows // 2 * heads
    return pl.pallas_call(
        functools.partial(backward_kernel, blocks),
        out_shape=jax.ShapeDtypeStruct((rows, heads * HEAD), BF),
        grid_spec=pltpu.PrefetchScalarGridSpec(
            num_scalar_prefetch=2,
            grid=(heads,),
            in_specs=[
                head_block(rows, DK),
                head_block(rows, DK),
                head_block(rows, DV),
                head_block(rows, DV),
                head_block(rows, DV, HEAD // DV, HEAD // DV - 1),
                head_block(rows, DV),
            ]
            + table_specs(rows),
            out_specs=head_block(rows, HEAD),
            scratch_shapes=[
                pltpu.VMEM((rows, DV), BF),
                pltpu.VMEM((rows, DK), F32),
                pltpu.VMEM((rows, DK), F32),
                pltpu.VMEM((rows, DV), F32),
            ],
        ),
        compiler_params=pltpu.CompilerParams(vmem_limit_bytes=56 << 20),
        cost_estimate=pl.CostEstimate(
            flops=pairs * (3 * DK + 2 * DV) * 2,
            transcendentals=pairs,
            bytes_accessed=rows * heads * (DK * 4 + DV * 14 + HEAD * 2),
        ),
        name="retention_backward",
    )(active, gammas, query, key, value, mixed, proj, grad_gated, *tables)


def on_device(
    block_input,
    cotangent,
    sequence_lengths,
    sequence_owner,
    sequence_offset,
    query_key,
    value_gate,
    output_weight,
    feed_in,
    feed_out,
    mean_query_key,
    mean_value_gate,
    mean_output_weight,
    mean_feed_in,
    mean_feed_out,
    square_query_key,
    square_value_gate,
    square_output_weight,
    square_feed_in,
    square_feed_out,
):
    tensors = lax.axis_size("tensor")
    local_rows = block_input.shape[0]
    heads = query_key.shape[2] // DK
    hidden = feed_in.shape[2]
    tensor_index = lax.axis_index("tensor")
    data_index = lax.axis_index("dp")

    block_ids = jnp.arange(tensors, dtype=jnp.int32) ^ tensor_index
    row_ids = (
        block_ids[:, None] * local_rows + jnp.arange(local_rows, dtype=jnp.int32)[None, :]
    ).reshape(-1)
    segment, position, valid = row_tables(
        sequence_lengths, sequence_owner, sequence_offset, data_index, row_ids
    )
    valid_here = valid[:local_rows].astype(F32)[:, None]
    cosine, sine = rotary_tables(position, DK // 2)
    head_ids = (tensor_index * heads + jnp.arange(heads, dtype=jnp.int32)).astype(F32)
    log_gamma = jnp.log(1.0 - jnp.exp2(-5.0 - head_ids))
    shaped = segment.reshape(tensors, local_rows)
    highest = jnp.max(shaped, axis=1)
    lowest = jnp.min(jnp.where(shaped >= 0, shaped, 1 << 30), axis=1)
    active = (
        (block_ids[None, :] <= block_ids[:, None]) & (highest[None, :] >= lowest[:, None])
    ).astype(jnp.int32).reshape(-1)
    tables = (
        cosine,
        sine,
        segment[:, None],
        position[:, None],
        segment[None, :],
        position[None, :],
    )

    pieces = []
    for h in range(heads):
        pieces += [
            query_key[0, :, h * DK : (h + 1) * DK],
            query_key[1, :, h * DK : (h + 1) * DK],
            value_gate[0, :, h * DV : (h + 1) * DV],
            value_gate[1, :, h * DV : (h + 1) * DV],
        ]
    weight_proj = lax.all_gather(
        jnp.concatenate(pieces, axis=1).astype(BF), "dp", axis=0, tiled=True
    )
    weight_out = lax.all_gather(output_weight.astype(BF), "dp", axis=1, tiled=True)
    weight_up = lax.all_gather(
        jnp.concatenate([feed_in[0], feed_in[1]], axis=1).astype(BF), "dp", axis=0, tiled=True
    )
    weight_down = lax.all_gather(feed_out.astype(BF), "dp", axis=1, tiled=True)

    inputs_f = block_input.astype(F32)
    in_scale = lax.rsqrt(jnp.mean(inputs_f * inputs_f, axis=1, keepdims=True) + EPS_NORM)
    rows_in = gather_blocks((inputs_f * in_scale).astype(BF), tensors)
    grad_out_f = cotangent.astype(F32)
    branch_rows = gather_blocks((valid_here * grad_out_f).astype(BF), tensors)
    proj = times(rows_in, weight_proj)
    query, key, value, mixed, gated = retention_forward(proj, tables, active, log_gamma, tensors)

    def rows_of(array, k):
        return array[k * local_rows : (k + 1) * local_rows]

    hidden_state = inputs_f + scatter_blocks(
        lambda k: times(rows_of(gated, k), weight_out), tensors
    )
    mid_scale = lax.rsqrt(jnp.mean(hidden_state * hidden_state, axis=1, keepdims=True) + EPS_NORM)
    rows_mid = gather_blocks((hidden_state * mid_scale).astype(BF), tensors)

    up = times(rows_mid, weight_up)
    up_gate = up[:, :hidden]
    up_line = up[:, hidden:]
    normal_cdf = 0.5 * (1.0 + lax.erf(up_gate / math.sqrt(2.0)))
    activated = up_gate * normal_cdf
    expanded = (activated * up_line).astype(BF)
    slope_down = lax.psum_scatter(
        contract_rows(expanded, branch_rows), "dp", scatter_dimension=1, tiled=True
    ).astype(F32)
    grad_expanded = times_t(branch_rows, weight_down)
    normal_pdf = 1.0 / math.sqrt(2.0 * math.pi) * jnp.exp(-0.5 * up_gate * up_gate)
    grad_up = jnp.concatenate(
        [
            (grad_expanded * up_line * (normal_cdf + up_gate * normal_pdf)).astype(BF),
            (grad_expanded * activated).astype(BF),
        ],
        axis=1,
    )
    grad_mid = scatter_blocks(lambda k: times_t(rows_of(grad_up, k), weight_up), tensors)
    slope_up = lax.psum_scatter(
        contract_rows(rows_mid, grad_up), "dp", scatter_dimension=0, tiled=True
    ).astype(F32)
    block_output = (
        hidden_state
        + valid_here * scatter_blocks(lambda k: times(rows_of(expanded, k), weight_down), tensors)
    ).astype(BF)

    grad_hidden = (
        grad_out_f
        + mid_scale * grad_mid
        - hidden_state * mid_scale**3 * jnp.mean(grad_mid * hidden_state, axis=1, keepdims=True)
    )
    grad_rows = gather_blocks(grad_hidden.astype(BF), tensors)
    slope_out = lax.psum_scatter(
        contract_rows(gated, grad_rows), "dp", scatter_dimension=1, tiled=True
    ).astype(F32)
    grad_gated = times_t(grad_rows, weight_out)
    grad_proj = retention_backward(
        query, key, value, mixed, proj, grad_gated, tables, active, log_gamma, tensors
    )
    slope_proj = lax.psum_scatter(
        contract_rows(rows_in, grad_proj), "dp", scatter_dimension=0, tiled=True
    ).astype(F32)
    grad_in = scatter_blocks(lambda k: times_t(rows_of(grad_proj, k), weight_proj), tensors)
    input_gradient = (
        grad_hidden
        + in_scale * grad_in
        - inputs_f * in_scale**3 * jnp.mean(grad_in * inputs_f, axis=1, keepdims=True)
    )

    def columns(start, width):
        return jnp.concatenate(
            [slope_proj[:, h * HEAD + start : h * HEAD + start + width] for h in range(heads)],
            axis=1,
        )

    slope_qk = jnp.stack([columns(0, DK), columns(DK, DK)])
    slope_vg = jnp.stack([columns(2 * DK, DV), columns(2 * DK + DV, DV)])
    slope_in = jnp.stack([slope_up[:, :hidden], slope_up[:, hidden:]])
    new_qk = adam_update(query_key, mean_query_key, square_query_key, slope_qk)
    new_vg = adam_update(value_gate, mean_value_gate, square_value_gate, slope_vg)
    new_out = adam_update(output_weight, mean_output_weight, square_output_weight, slope_out)
    new_in = adam_update(feed_in, mean_feed_in, square_feed_in, slope_in)
    new_down = adam_update(feed_out, mean_feed_out, square_feed_out, slope_down)
    return (
        block_output,
        input_gradient,
        slope_qk,
        slope_vg,
        slope_out,
        slope_in,
        slope_down,
        new_qk[0],
        new_vg[0],
        new_out[0],
        new_in[0],
        new_down[0],
        new_qk[1],
        new_vg[1],
        new_out[1],
        new_in[1],
        new_down[1],
        new_qk[2],
        new_vg[2],
        new_out[2],
        new_in[2],
        new_down[2],
    )


def solution(mesh):
    rows = P(("dp", "tensor"), None)
    stacked = P(None, "dp", "tensor")
    turned = P("tensor", "dp")
    weights = (stacked, stacked, turned, stacked, turned)
    return jax.shard_map(
        on_device,
        mesh=mesh,
        in_specs=(rows, rows, P(), P(), P()) + weights * 3,
        out_specs=(rows, rows) + weights * 4,
        check_vma=False,
    )
```

```python
import functools
import math

import jax
import jax.numpy as jnp
from jax import lax
from jax.experimental import pallas as pl
from jax.experimental.pallas import tpu as pltpu
from jax.sharding import PartitionSpec as P


DK = 256
DV = 512
HEAD = 2 * DK + 2 * DV

EPS_NORM = 1e-06
EPS_GROUP = 1e-05
LEARN_RATE = 0.01
BETA_FIRST = 0.9
BETA_SECOND = 0.999
ADAM_EPS = 1e-08
WEIGHT_DECAY = 0.1
step_count = 3


BF = jnp.bfloat16
F32 = jnp.float32


def row_tables(lengths, owners, offsets, buffer, rows):
    numbers = jnp.arange(lengths.shape[0], dtype=jnp.int32)
    inside = (
        (owners[None, :] == buffer)
        & (rows[:, None] >= offsets[None, :])
        & (rows[:, None] < offsets[None, :] + lengths[None, :])
    )
    inside = inside.astype(jnp.int32)
    segment = jnp.sum(inside * (numbers[None, :] + 1), axis=1) - 1
    position = jnp.sum(inside * (rows[:, None] - offsets[None, :]), axis=1)
    valid = jnp.sum(inside, axis=1)
    return (segment, position, valid)


def rotary_tables(position, half):
    ladder = jnp.exp(-math.log(10000.0) * jnp.arange(half, dtype=F32) / half)
    angle = position.astype(F32)[:, None] * ladder[None, :]
    return (jnp.cos(angle), jnp.sin(angle))


def contract_rows(left, right, kind=BF):
    return lax.dot_general(
        left, right, (((0,), (0,)), ((), ())), preferred_element_type=F32
    ).astype(kind)


def times(left, right):
    return lax.dot_general(left, right, (((1,), (0,)), ((), ())), preferred_element_type=F32)


def times_t(left, right):
    return lax.dot_general(left, right, (((1,), (1,)), ((), ())), preferred_element_type=F32)


def adam_update(weight, first, second, slope):
    weight = after(weight, slope)
    first_new = BETA_FIRST * first + (1.0 - BETA_FIRST) * slope
    second_new = BETA_SECOND * second + (1.0 - BETA_SECOND) * slope * slope
    first_hat = first_new / (1.0 - BETA_FIRST**step_count)
    second_hat = second_new / (1.0 - BETA_SECOND**step_count)
    weight_new = weight - LEARN_RATE * (
        first_hat / (jnp.sqrt(second_hat) + ADAM_EPS) + WEIGHT_DECAY * weight
    )
    return (weight_new, first_new, second_new)


def swap(block, k, tensors):
    return lax.ppermute(block, "tensor", [(i, i ^ k) for i in range(tensors)])


def after(value, *others):
    return lax.optimization_barrier((value,) + others)[0]


def gather_blocks(block, tensors):
    if tensors != 4:
        got = {k: swap(block, k, tensors) for k in range(tensors - 1, 0, -1)}
        return [block] + [got[k] for k in range(1, tensors)]
    cut = block.shape[0] // 2
    one = swap(block, 1, tensors)
    two = swap(block, 2, tensors)
    top = swap(two[:cut], 1, tensors)
    low = swap(one[cut:], 2, tensors)
    return [block, one, two, top, low]


def scatter_blocks(make, tensors, last=()):
    if tensors != 4:
        got = [swap(make(k).astype(BF), k, tensors) for k in range(tensors - 1, 0, -1)]
        total = after(make(0).astype(BF), *last).astype(F32)
        for part in got:
            total = total + part.astype(F32)
        return total
    far = make(3).astype(BF)
    cut = far.shape[0] // 2
    one = make(1).astype(BF)
    two = make(2).astype(BF)
    far_x = swap(far[:cut], 1, tensors)
    far_y = swap(far[cut:], 2, tensors)
    one_x = swap(one[:cut], 1, tensors)
    two_y = swap(two[cut:], 2, tensors)
    own = after(make(0).astype(BF), *last)
    top_y = swap((two[:cut].astype(F32) + far_x.astype(F32)).astype(BF), 2, tensors)
    low_x = swap((one[cut:].astype(F32) + far_y.astype(F32)).astype(BF), 1, tensors)
    top = own[:cut].astype(F32) + one_x.astype(F32) + top_y.astype(F32)
    low = own[cut:].astype(F32) + two_y.astype(F32) + low_x.astype(F32)
    return jnp.concatenate([top, low], axis=0)


def decay_of(seg_rows, pos_rows, seg_cols, pos_cols, log_gamma):
    linked = (seg_rows == seg_cols) & (seg_rows >= 0) & (pos_cols <= pos_rows)
    spacing = jnp.maximum(pos_rows - pos_cols, 0).astype(F32)
    return jnp.where(linked, jnp.exp(spacing * log_gamma), 0.0)


def forward_kernel(blocks, active, gammas, proj, cos, sin, segc, posc, segr, posr,
                   query, key, value, mixed, gated):
    size = proj.shape[0] // blocks
    half = DK // 2
    log_gamma = gammas[pl.program_id(0)]

    def spin(index, carry):
        rows = pl.ds(pl.multiple_of(index * size, size), size)
        c = cos[rows, :]
        s = sin[rows, :]
        a = proj[rows, 0:half]
        b = proj[rows, half:DK]
        query[rows, 0:half] = (a * c - b * s).astype(BF)
        query[rows, half:DK] = (b * c + a * s).astype(BF)
        a = proj[rows, DK : DK + half]
        b = proj[rows, DK + half : 2 * DK]
        key[rows, 0:half] = ((a * c - b * s) * DK ** (-0.5)).astype(BF)
        key[rows, half:DK] = ((b * c + a * s) * DK ** (-0.5)).astype(BF)
        value[rows, :] = proj[rows, 2 * DK : 2 * DK + DV].astype(BF)
        mixed[rows, :] = jnp.zeros((size, DV), F32)
        return carry

    lax.fori_loop(0, blocks, spin, 0)

    def query_block(qi, carry):
        rows = pl.ds(pl.multiple_of(qi * size, size), size)
        for ki in range(blocks):
            cols = slice(ki * size, (ki + 1) * size)

            @pl.when(active[qi * blocks + ki] != 0)
            def _():
                decay = decay_of(
                    segc[rows, :], posc[rows, :], segr[:, cols], posr[:, cols], log_gamma
                )
                scores = (times_t(query[rows, :], key[cols, :]) * decay).astype(BF)
                mixed[rows, :] += times(scores, value[cols, :])

        total = mixed[rows, :]
        scale = lax.rsqrt(jnp.mean(total * total, axis=1, keepdims=True) + EPS_GROUP)
        gate = proj[rows, 2 * DK + DV : HEAD]
        gated[rows, :] = (gate * jax.nn.sigmoid(gate) * (total * scale)).astype(BF)
        return carry

    lax.fori_loop(0, blocks, query_block, 0)


def backward_kernel(blocks, active, gammas, query, key, value, mixed, gate_ref, grad_gated,
                    cos, sin, segc, posc, segr, posr, out, grad_mixed, grad_q, grad_k, grad_v):
    size = query.shape[0] // blocks
    half = DK // 2
    log_gamma = gammas[pl.program_id(0)]

    def prepare(index, carry):
        rows = pl.ds(pl.multiple_of(index * size, size), size)
        total = mixed[rows, :]
        gate = gate_ref[rows, :]
        slope = grad_gated[rows, :]
        scale = lax.rsqrt(jnp.mean(total * total, axis=1, keepdims=True) + EPS_GROUP)
        sigma = jax.nn.sigmoid(gate)
        out[rows, 2 * DK + DV : HEAD] = (
            slope * (total * scale) * sigma * (1.0 + gate * (1.0 - sigma))
        ).astype(BF)
        normed = slope * (gate * sigma)
        grad_mixed[rows, :] = (
            scale * normed
            - total * (scale * scale * scale) * jnp.mean(normed * total, axis=1, keepdims=True)
        ).astype(BF)
        grad_q[rows, :] = jnp.zeros((size, DK), F32)
        grad_k[rows, :] = jnp.zeros((size, DK), F32)
        grad_v[rows, :] = jnp.zeros((size, DV), F32)
        return carry

    lax.fori_loop(0, blocks, prepare, 0)

    def query_block(qi, carry):
        rows = pl.ds(pl.multiple_of(qi * size, size), size)
        for ki in range(blocks):
            cols = slice(ki * size, (ki + 1) * size)

            @pl.when(active[qi * blocks + ki] != 0)
            def _():
                decay = decay_of(
                    segc[rows, :], posc[rows, :], segr[:, cols], posr[:, cols], log_gamma
                )
                q = query[rows, :]
                k = key[cols, :]
                slope = grad_mixed[rows, :]
                scores = (times_t(q, k) * decay).astype(BF)
                grad_scores = (times_t(slope, value[cols, :]) * decay).astype(BF)
                grad_q[rows, :] += times(grad_scores, k)
                grad_k[cols, :] += contract_rows(grad_scores, q, F32)
                grad_v[cols, :] += contract_rows(scores, slope, F32)

        return carry

    lax.fori_loop(0, blocks, query_block, 0)

    def finish(index, carry):
        rows = pl.ds(pl.multiple_of(index * size, size), size)
        c = cos[rows, :]
        s = sin[rows, :]
        a = grad_q[rows, 0:half]
        b = grad_q[rows, half:DK]
        out[rows, 0:half] = (a * c + b * s).astype(BF)
        out[rows, half:DK] = (b * c - a * s).astype(BF)
        a = grad_k[rows, 0:half]
        b = grad_k[rows, half:DK]
        out[rows, DK : DK + half] = ((a * c + b * s) * DK ** (-0.5)).astype(BF)
        out[rows, DK + half : 2 * DK] = ((b * c - a * s) * DK ** (-0.5)).astype(BF)
        out[rows, 2 * DK : 2 * DK + DV] = grad_v[rows, :].astype(BF)
        return carry

    lax.fori_loop(0, blocks, finish, 0)


def whole_block(shape):
    return pl.BlockSpec(shape, lambda h, *_: (0, 0))


def head_block(rows, width, scale=1, shift=0):
    return pl.BlockSpec((rows, width), lambda h, *_: (0, h * scale + shift))


def table_specs(rows):
    return [
        whole_block((rows, DK // 2)),
        whole_block((rows, DK // 2)),
        whole_block((rows, 1)),
        whole_block((rows, 1)),
        whole_block((1, rows)),
        whole_block((1, rows)),
    ]


def retention_forward(proj, tables, active, gammas, blocks):
    rows, width = proj.shape
    heads = width // HEAD
    pairs = rows * rows // 2 * heads
    return pl.pallas_call(
        functools.partial(forward_kernel, blocks),
        out_shape=(
            jax.ShapeDtypeStruct((rows, heads * DK), BF),
            jax.ShapeDtypeStruct((rows, heads * DK), BF),
            jax.ShapeDtypeStruct((rows, heads * DV), BF),
            jax.ShapeDtypeStruct((rows, heads * DV), F32),
            jax.ShapeDtypeStruct((rows, heads * DV), BF),
        ),
        grid_spec=pltpu.PrefetchScalarGridSpec(
            num_scalar_prefetch=2,
            grid=(heads,),
            in_specs=[head_block(rows, HEAD)] + table_specs(rows),
            out_specs=(
                head_block(rows, DK),
                head_block(rows, DK),
                head_block(rows, DV),
                head_block(rows, DV),
                head_block(rows, DV),
            ),
        ),
        compiler_params=pltpu.CompilerParams(vmem_limit_bytes=56 << 20),
        cost_estimate=pl.CostEstimate(
            flops=pairs * (DK + DV) * 2,
            transcendentals=pairs,
            bytes_accessed=rows * heads * (HEAD * 4 + DK * 4 + DV * 8),
        ),
        name="retention_forward",
    )(active, gammas, proj, *tables)


def retention_backward(query, key, value, mixed, proj, grad_gated, tables, active, gammas, blocks):
    rows = query.shape[0]
    heads = query.shape[1] // DK
    pairs = rows * rows // 2 * heads
    return pl.pallas_call(
        functools.partial(backward_kernel, blocks),
        out_shape=jax.ShapeDtypeStruct((rows, heads * HEAD), BF),
        grid_spec=pltpu.PrefetchScalarGridSpec(
            num_scalar_prefetch=2,
            grid=(heads,),
            in_specs=[
                head_block(rows, DK),
                head_block(rows, DK),
                head_block(rows, DV),
                head_block(rows, DV),
                head_block(rows, DV, HEAD // DV, HEAD // DV - 1),
                head_block(rows, DV),
            ]
            + table_specs(rows),
            out_specs=head_block(rows, HEAD),
            scratch_shapes=[
                pltpu.VMEM((rows, DV), BF),
                pltpu.VMEM((rows, DK), F32),
                pltpu.VMEM((rows, DK), F32),
                pltpu.VMEM((rows, DV), F32),
            ],
        ),
        compiler_params=pltpu.CompilerParams(vmem_limit_bytes=56 << 20),
        cost_estimate=pl.CostEstimate(
            flops=pairs * (3 * DK + 2 * DV) * 2,
            transcendentals=pairs,
            bytes_accessed=rows * heads * (DK * 4 + DV * 14 + HEAD * 2),
        ),
        name="retention_backward",
    )(active, gammas, query, key, value, mixed, proj, grad_gated, *tables)


def on_device(
    block_input,
    cotangent,
    sequence_lengths,
    sequence_owner,
    sequence_offset,
    query_key,
    value_gate,
    output_weight,
    feed_in,
    feed_out,
    mean_query_key,
    mean_value_gate,
    mean_output_weight,
    mean_feed_in,
    mean_feed_out,
    square_query_key,
    square_value_gate,
    square_output_weight,
    square_feed_in,
    square_feed_out,
):
    tensors = lax.axis_size("tensor")
    local_rows = block_input.shape[0]
    heads = query_key.shape[2] // DK
    hidden = feed_in.shape[2]
    tensor_index = lax.axis_index("tensor")
    data_index = lax.axis_index("dp")

    block_ids = jnp.arange(tensors, dtype=jnp.int32) ^ tensor_index
    row_ids = (
        block_ids[:, None] * local_rows + jnp.arange(local_rows, dtype=jnp.int32)[None, :]
    ).reshape(-1)
    segment, position, valid = row_tables(
        sequence_lengths, sequence_owner, sequence_offset, data_index, row_ids
    )
    valid_here = valid[:local_rows].astype(F32)[:, None]
    cosine, sine = rotary_tables(position, DK // 2)
    head_ids = (tensor_index * heads + jnp.arange(heads, dtype=jnp.int32)).astype(F32)
    log_gamma = jnp.log(1.0 - jnp.exp2(-5.0 - head_ids))
    shaped = segment.reshape(tensors, local_rows)
    highest = jnp.max(shaped, axis=1)
    lowest = jnp.min(jnp.where(shaped >= 0, shaped, 1 << 30), axis=1)
    active = (
        (block_ids[None, :] <= block_ids[:, None]) & (highest[None, :] >= lowest[:, None])
    ).astype(jnp.int32).reshape(-1)
    tables = (
        cosine,
        sine,
        segment[:, None],
        position[:, None],
        segment[None, :],
        position[None, :],
    )

    pieces = []
    for h in range(heads):
        pieces += [
            query_key[0, :, h * DK : (h + 1) * DK],
            query_key[1, :, h * DK : (h + 1) * DK],
            value_gate[0, :, h * DV : (h + 1) * DV],
            value_gate[1, :, h * DV : (h + 1) * DV],
        ]
    weight_proj = lax.all_gather(
        jnp.concatenate(pieces, axis=1).astype(BF), "dp", axis=0, tiled=True
    )
    weight_out = lax.all_gather(output_weight.astype(BF), "dp", axis=1, tiled=True)
    weight_up = lax.all_gather(
        jnp.concatenate([feed_in[0], feed_in[1]], axis=1).astype(BF), "dp", axis=0, tiled=True
    )
    weight_down = lax.all_gather(feed_out.astype(BF), "dp", axis=1, tiled=True)

    inputs_f = block_input.astype(F32)
    in_scale = lax.rsqrt(jnp.mean(inputs_f * inputs_f, axis=1, keepdims=True) + EPS_NORM)
    rows_in = jnp.concatenate(gather_blocks((inputs_f * in_scale).astype(BF), tensors), axis=0)
    grad_out_f = cotangent.astype(F32)
    grad_branch = (valid_here * grad_out_f).astype(BF)
    branch_rows = jnp.concatenate(
        gather_blocks(after(grad_branch, rows_in), tensors), axis=0
    )
    proj = times(after(rows_in, branch_rows), weight_proj)
    query, key, value, mixed, gated = retention_forward(proj, tables, active, log_gamma, tensors)

    def rows_of(array, k):
        return array[k * local_rows : (k + 1) * local_rows]

    hidden_state = inputs_f + scatter_blocks(
        lambda k: times(rows_of(gated, k), weight_out), tensors
    )
    mid_scale = lax.rsqrt(jnp.mean(hidden_state * hidden_state, axis=1, keepdims=True) + EPS_NORM)
    rows_mid = jnp.concatenate(
        gather_blocks((hidden_state * mid_scale).astype(BF), tensors), axis=0
    )

    up = times(rows_mid, weight_up)
    up_gate = up[:, :hidden]
    up_line = up[:, hidden:]
    normal_cdf = 0.5 * (1.0 + lax.erf(up_gate / math.sqrt(2.0)))
    activated = up_gate * normal_cdf
    expanded = lax.optimization_barrier((activated * up_line).astype(BF))
    part_down = contract_rows(expanded, branch_rows)
    slope_down = lax.psum_scatter(part_down, "dp", scatter_dimension=1, tiled=True).astype(F32)
    grad_expanded = times_t(after(branch_rows, part_down), weight_down)
    normal_pdf = 1.0 / math.sqrt(2.0 * math.pi) * jnp.exp(-0.5 * up_gate * up_gate)
    grad_up = jnp.concatenate(
        [
            (grad_expanded * up_line * (normal_cdf + up_gate * normal_pdf)).astype(BF),
            (grad_expanded * activated).astype(BF),
        ],
        axis=1,
    )
    part_up = contract_rows(rows_mid, grad_up)
    slope_up = lax.psum_scatter(part_up, "dp", scatter_dimension=0, tiled=True).astype(F32)
    grad_mid = scatter_blocks(
        lambda k: times_t(rows_of(grad_up, k), weight_up), tensors, last=(part_up,)
    )

    grad_hidden = (
        grad_out_f
        + mid_scale * grad_mid
        - hidden_state * mid_scale**3 * jnp.mean(grad_mid * hidden_state, axis=1, keepdims=True)
    )
    grad_block = grad_hidden.astype(BF)
    grad_parts = gather_blocks(grad_block, tensors)
    held = after(expanded, grad_block)
    grad_rows = jnp.concatenate(grad_parts, axis=0)
    block_output = (
        hidden_state
        + valid_here
        * scatter_blocks(
            lambda k: after(
                times(rows_of(held, k), weight_down).astype(BF), *grad_parts[1:]
            ),
            tensors,
        )
    ).astype(BF)
    part_out = contract_rows(gated, grad_rows)
    slope_out = lax.psum_scatter(part_out, "dp", scatter_dimension=1, tiled=True).astype(F32)
    grad_gated = times_t(after(grad_rows, part_out), weight_out)
    grad_proj = retention_backward(
        query, key, value, mixed, proj, grad_gated, tables, active, log_gamma, tensors
    )
    part_proj = contract_rows(rows_in, grad_proj)
    slope_proj = lax.psum_scatter(part_proj, "dp", scatter_dimension=0, tiled=True).astype(F32)
    held_proj = after(grad_proj, part_proj)
    grad_in = scatter_blocks(lambda k: times_t(rows_of(held_proj, k), weight_proj), tensors)
    input_gradient = (
        grad_hidden
        + in_scale * grad_in
        - inputs_f * in_scale**3 * jnp.mean(grad_in * inputs_f, axis=1, keepdims=True)
    )

    def columns(start, width):
        return jnp.concatenate(
            [slope_proj[:, h * HEAD + start : h * HEAD + start + width] for h in range(heads)],
            axis=1,
        )

    slope_qk = jnp.stack([columns(0, DK), columns(DK, DK)])
    slope_vg = jnp.stack([columns(2 * DK, DV), columns(2 * DK + DV, DV)])
    slope_in = jnp.stack([slope_up[:, :hidden], slope_up[:, hidden:]])
    new_qk = adam_update(query_key, mean_query_key, square_query_key, slope_qk)
    new_vg = adam_update(value_gate, mean_value_gate, square_value_gate, slope_vg)
    new_out = adam_update(output_weight, mean_output_weight, square_output_weight, slope_out)
    new_in = adam_update(feed_in, mean_feed_in, square_feed_in, slope_in)
    new_down = adam_update(feed_out, mean_feed_out, square_feed_out, slope_down)
    return (
        block_output,
        input_gradient,
        slope_qk,
        slope_vg,
        slope_out,
        slope_in,
        slope_down,
        new_qk[0],
        new_vg[0],
        new_out[0],
        new_in[0],
        new_down[0],
        new_qk[1],
        new_vg[1],
        new_out[1],
        new_in[1],
        new_down[1],
        new_qk[2],
        new_vg[2],
        new_out[2],
        new_in[2],
        new_down[2],
    )


def solution(mesh):
    rows = P(("dp", "tensor"), None)
    stacked = P(None, "dp", "tensor")
    turned = P("tensor", "dp")
    weights = (stacked, stacked, turned, stacked, turned)

    return jax.shard_map(
        on_device,
        mesh=mesh,
        in_specs=(rows, rows, P(), P(), P()) + weights * 3,
        out_specs=(rows, rows) + weights * 4,
        check_vma=False,
    )
```
